32 devices in a mesh: seq: 8 (over z, y), tensor: 4 (over x, core).
Axes of the slice: x: 2, y: 2, z: 4, core: 2. Of those that a mesh axis runs over, the one named last changes fastest.
Arguments:
- tokens: bfloat16 [8192, 1024], P('seq'), may hold values from -6 to 6
- norm_in: bfloat16 [1024], replicated, may hold values from 0.5 to 1.5
- w_in: bfloat16 [1024, 3, 1024], P(None, None, 'tensor'), may hold values from -0.1875 to 0.1875
- conv_weight: bfloat16 [3, 1024], P(None, 'tensor'), may hold values from -3.5 to 3.5
- w_out: bfloat16 [1024, 1024], P('tensor'), may hold values from -0.1875 to 0.1875
- norm_ffn: bfloat16 [1024], replicated, may hold values from 0.5 to 1.5
- w_gate_up: bfloat16 [1024, 2, 4608], P(None, None, 'tensor'), may hold values from -0.1875 to 0.1875
- w_down: bfloat16 [4608, 1024], P('tensor'), may hold values from -0.09375 to 0.09375
- cotangent: bfloat16 [8192, 1024], P('seq'), may hold values from -6 to 6
Outputs:
- layer_out: bfloat16 [8192, 1024], P('seq')
- grad_tokens: bfloat16 [8192, 1024], P('seq')
- grad_norm_in: float32 [1024], replicated
- grad_norm_ffn: float32 [1024], replicated
- grad_w_in: float32 [1024, 3, 1024], P(None, None, 'tensor')
- grad_conv: float32 [3, 1024], P(None, 'tensor')
- grad_w_out: float32 [1024, 1024], P('tensor')
- grad_gate_up: float32 [1024, 2, 4608], P(None, None, 'tensor')
- grad_down: float32 [4608, 1024], P('tensor')
The draws below stay inside these ranges and needn't reach their ends.
All inputs are finite; a program needn't handle non-finite values.
Results may differ from the reference program's by a relative error of at most 0.024.
Values may be sent and summed in bfloat16 or wider, within the bound.
No kernel may reach another device: no remote copies, remote signals or barrier semaphores. Data moves between devices by JAX's collectives and lax.ppermute only.
A program may use at most 192 MiB of HBM per device.

```python
import jax
import jax.numpy as jnp
from jax import lax

D = 1024
FF = 4608
KERNEL = 3
TOKENS = 8192
LENGTH = 8192
N_TENSOR = 4


def block_levels(key, shape, pieces, least, top_value):
    loudness = 1.0
    for dim, parts in pieces:
        draws = jax.random.uniform(jax.random.fold_in(jax.random.fold_in(key, 6), dim), (parts,), jnp.float32, least / len(pieces), top_value / len(pieces))
        loudness = loudness * jnp.repeat(jnp.exp(draws), shape[dim] // parts).reshape((-1,) + (1,) * (len(shape) - 1 - dim))
    return loudness


def centred(own_key, extent, spread, bound, pieces=(), held_as=jnp.bfloat16):
    values = jax.random.normal(own_key, extent, jnp.float32) * spread
    if len(pieces) > 0:
        values = block_levels(own_key, extent, pieces, -0.22, 0.18) * values
    return jnp.clip(values, min=-bound, max=bound).astype(held_as)


def setup_inputs(seed: int = 0) -> dict:
    arg_keys = jax.random.split(jax.random.key(seed), 10)
    tokens = centred(arg_keys[0], (TOKENS, D), 1.0, 6.0, ((0, 8),))
    norm_in = jnp.clip(1.0 + 0.1 * jax.random.normal(arg_keys[1], (D,), jnp.float32), 0.5, 1.5).astype(jnp.bfloat16)
    w_in = centred(arg_keys[2], (D, 3, D), D ** -0.5, 0.1875, ((2, 4),))
    conv_weight = centred(arg_keys[3], (KERNEL, D), KERNEL ** -0.5, 3.5, ((1, 4),))
    w_out = centred(arg_keys[4], (D, D), D ** -0.5, 0.1875, ((0, 4),))
    norm_ffn = jnp.clip(1.0 + 0.1 * jax.random.normal(arg_keys[5], (D,), jnp.float32), 0.5, 1.5).astype(jnp.bfloat16)
    w_gate_up = centred(arg_keys[6], (D, 2, FF), D ** -0.5, 0.1875, ((2, 4),))
    w_down = centred(arg_keys[7], (FF, D), FF ** -0.5, 0.09375, ((0, 4),))
    cotangent = centred(arg_keys[8], (TOKENS, D), 1.0, 6.0, ((0, 8),))
    return {"tokens": tokens, "norm_in": norm_in, "w_in": w_in, "conv_weight": conv_weight, "w_out": w_out, "norm_ffn": norm_ffn, "w_gate_up": w_gate_up, "w_down": w_down, "cotangent": cotangent}


EPSILON = 1e-05
HIGHEST_PREC = lax.Precision.HIGHEST

@jax.custom_vjp
def low(v):
    return lax.optimization_barrier(v.astype(jnp.bfloat16)).astype(jnp.float32)

@jax.custom_vjp
def low_back(v):
    return v

def low_keep(v):
    return (low(v), None)

def low_pass(kept, grad):
    return (grad,)

def back_keep(v):
    return (v, None)

def back_low(kept, grad):
    return (low(grad),)
low.defvjp(low_keep, low_pass)
low_back.defvjp(back_keep, back_low)

def norm_rows(stream, gain):
    factor = lax.rsqrt(lax.optimization_barrier(jnp.mean(stream * stream, axis=-1, keepdims=True)) + EPSILON)
    return stream * factor * gain

def layer(stream, norm_in, w_in, conv_weight, w_out, norm_ffn, w_gate_up, w_down):
    groups = N_TENSOR
    width = w_in.shape[0]
    channels = width // groups
    ff_width = w_down.shape[0]
    ff_group = ff_width // groups
    normed = low(norm_rows(stream, norm_in))
    copies = low_back(jnp.broadcast_to(normed[None], (groups,) + normed.shape))
    projected = low_back(jnp.einsum('gtd,dkgc->gtkc', copies, w_in.reshape(width, 3, groups, channels), precision=HIGHEST_PREC))
    gate_b = projected[:, :, 0]
    gate_c = projected[:, :, 1]
    values = projected[:, :, 2]
    product = low(gate_b * values)
    padded = jnp.pad(product, ((0, 0), (2, 0), (0, 0)))
    taps = conv_weight.reshape(3, groups, channels)
    conv_out = taps[0][:, None, :] * padded[:, :-2] + taps[1][:, None, :] * padded[:, 1:-1] + taps[2][:, None, :] * padded[:, 2:]
    conv_out = low_back(conv_out)
    gated = low(gate_c * conv_out)
    partial_value = low(jnp.einsum('gtc,gcd->gtd', gated, w_out.reshape(groups, channels, width), precision=HIGHEST_PREC))
    branch = low_back(lax.optimization_barrier(jnp.sum(partial_value, axis=0)))
    middle = stream + branch
    normed_ffn = low(norm_rows(middle, norm_ffn))
    copies_ffn = low_back(jnp.broadcast_to(normed_ffn[None], (groups,) + normed_ffn.shape))
    gate_up = low_back(jnp.einsum('gtd,dkgf->gtkf', copies_ffn, w_gate_up.reshape(width, 2, groups, ff_group), precision=HIGHEST_PREC))
    activated = low(jax.nn.silu(gate_up[:, :, 0]) * gate_up[:, :, 1])
    partial_ffn = low(jnp.einsum('gtf,gfd->gtd', activated, w_down.reshape(groups, ff_group, width), precision=HIGHEST_PREC))
    return middle + lax.optimization_barrier(jnp.sum(partial_ffn, axis=0))

def reference(tokens, norm_in, w_in, conv_weight, w_out, norm_ffn, w_gate_up, w_down, cotangent):
    count = TOKENS // LENGTH
    weights = tuple((item.astype(jnp.float32) for item in (norm_in, w_in, conv_weight, w_out, norm_ffn, w_gate_up, w_down)))
    inputs = tokens.astype(jnp.float32).reshape(count, LENGTH, D)
    cotans = cotangent.astype(jnp.float32).reshape(count, LENGTH, D)

    def one_sequence(totals, pair):
        seq_in, seq_cot = pair
        output, puller = jax.vjp(layer, seq_in, *weights)
        grads = puller(seq_cot)
        totals = tuple((total + grad for total, grad in zip(totals, grads[1:])))
        return (totals, (output.astype(jnp.bfloat16), grads[0].astype(jnp.bfloat16)))
    start_totals = tuple((jnp.zeros(item.shape, jnp.float32) for item in weights))
    totals, (outputs, grad_inputs) = lax.scan(one_sequence, start_totals, (inputs, cotans))
    return (outputs.reshape(TOKENS, D), grad_inputs.reshape(TOKENS, D), totals[0], totals[4], totals[1], totals[2], totals[3], totals[5], totals[6])
```

```python
import jax
import jax.numpy as jnp
from jax import lax
from jax.sharding import PartitionSpec as P

SEQ_LEN = 8192
EPSILON = 1e-05
F32 = jnp.float32
BF16 = jnp.bfloat16


def swap_pair(block, lines=None):
    n = lax.axis_size("seq")
    lines = range(n // 2) if lines is None else lines
    return lax.ppermute(block, "seq", [(2 * z + p, 2 * z + 1 - p) for z in lines for p in (0, 1)])


def along_line(block, route):
    return lax.ppermute(block, "seq", [(2 * a + p, 2 * b + p) for a, b in route for p in (0, 1)])


def swap_core(block):
    n = lax.axis_size("tensor")
    return lax.ppermute(block, "tensor", [(i, i ^ 1) for i in range(n)])


def swap_chip(block):
    n = lax.axis_size("tensor")
    return lax.ppermute(block, "tensor", [(i, i ^ 2) for i in range(n)])


def neighbour(block, distance):
    devices = range(lax.axis_size("seq"))
    route = [(i - distance, i) for i in devices if i - distance in devices]
    return lax.ppermute(block, "seq", route)


def add_low(a, b):
    return (a.astype(F32) + b.astype(F32)).astype(BF16)


def tie(value, after):
    value, after = lax.optimization_barrier((value, after))
    return value


INWARD, MIDDLE, OUTWARD = [(0, 1), (3, 2)], [(1, 2), (2, 1)], [(1, 0), (2, 3)]


def is_middle():
    line = lax.axis_index("seq") // 2
    return (line == 1) | (line == 2)


def butterfly(block):
    bit = 1
    while bit < lax.axis_size("seq") // 2:
        n = lax.axis_size("seq") // 2
        block = add_low(block, along_line(block, [(i, i ^ bit) for i in range(n)]))
        bit *= 2
    return block


class Lines:
    def __init__(self):
        self.first = []

    def send_in(self, block):
        if len(self.first) >= 2:
            block = tie(block, self.first[-2])
        got = along_line(block, INWARD)
        self.first.append(got)
        return add_low(block, got)

    def total(self, block):
        if lax.axis_size("seq") // 2 != 4:
            return butterfly(block)
        mid = self.send_in(block)
        full = add_low(mid, along_line(mid, MIDDLE))
        return jnp.where(is_middle(), full, along_line(full, OUTWARD))

    def total_pairs(self, block):
        if lax.axis_size("seq") // 2 != 4:
            block = butterfly(block)
            return add_low(block, swap_pair(block))
        half = block.shape[0] // 2
        low = lax.axis_index("seq") // 2 < 2
        mid = self.send_in(block)
        keep = jnp.where(low, mid[:half], mid[half:])
        send = jnp.where(low, mid[half:], mid[:half])
        part = add_low(keep, along_line(send, MIDDLE))
        part = add_low(part, swap_pair(part, (1, 2)))
        rest = along_line(part, MIDDLE)
        full = jnp.concatenate([jnp.where(low, part, rest), jnp.where(low, rest, part)], axis=0)
        return jnp.where(is_middle(), full, along_line(full, OUTWARD))


def dot(a, b):
    return jnp.dot(a, b, preferred_element_type=F32)


def dot_rows(a, b):
    return lax.dot_general(a, b, (((0,), (0,)), ((), ())), preferred_element_type=F32)


def dot_cols(a, b):
    return lax.dot_general(a, b, (((1,), (1,)), ((), ())), preferred_element_type=F32)


def inverse_rms(stream):
    return lax.rsqrt(jnp.mean(stream * stream, axis=-1, keepdims=True) + EPSILON)


def gates(normed, grad_out, w_gate, w_up, w_down):
    gate = dot(normed, w_gate)
    up = dot(normed, w_up)
    grad_act = dot_cols(grad_out, w_down)
    sig = jax.nn.sigmoid(gate)
    silu = gate * sig
    act = (silu * up).astype(BF16)
    grad_gate = (grad_act * up * sig * (1.0 + gate * (1.0 - sig))).astype(BF16)
    grad_up = (grad_act * silu).astype(BF16)
    return act, grad_gate, grad_up


def norm_back(grad, unit, factor, gain):
    scaled = grad * gain
    back = factor * (scaled - unit * jnp.mean(scaled * unit, axis=-1, keepdims=True))
    return back, jnp.sum(grad * unit, axis=0)


def shards(tokens, norm_in, w_in, conv_weight, w_out, norm_ffn, w_gate_up, w_down, cotangent):
    rows, width = tokens.shape
    half = rows // 2
    n_seq = lax.axis_size("seq")
    span = min(SEQ_LEN, rows * n_seq) // rows
    place = lax.axis_index("seq")
    starts_seq = place % span == 0
    ends_seq = place % span == span - 1
    pair = place % 2
    core = lax.axis_index("tensor") % 2
    first_core = core == 0

    def mine(block):
        return lax.dynamic_slice_in_dim(block, core * half, half, 0)

    def other(block):
        return lax.dynamic_slice_in_dim(block, (1 - core) * half, half, 0)

    def in_order(own, theirs):
        return jnp.concatenate(
            [jnp.where(first_core, own, theirs), jnp.where(first_core, theirs, own)], axis=0
        )

    def chip_sum(partial):
        chip = add_low(partial[:half], swap_core(partial[half:]))
        return chip.astype(F32) + swap_chip(chip).astype(F32)

    gain_in = norm_in.astype(F32)
    gain_ffn = norm_ffn.astype(F32)
    taps = conv_weight.astype(F32)

    cot_own, cot_other = mine(cotangent), other(cotangent)
    halo_tokens = neighbour(tokens[-16:], 1)
    w_out_chip = swap_chip(w_out)
    w_out_core = swap_core(w_out)
    cot_pair_own = swap_pair(cot_own)
    w_out_chip_core = swap_core(w_out_chip)
    cot_pair_other = swap_core(cot_pair_own)
    w_gate, w_up = w_gate_up[:, 0], w_gate_up[:, 1]

    inputs = tokens.astype(F32)
    scale_in = inverse_rms(inputs)
    normed = (inputs * scale_in * gain_in).astype(BF16)
    projected = jnp.einsum("td,dkc->tkc", normed, w_in, preferred_element_type=F32)
    gate_b, gate_c, values = projected[:, 0], projected[:, 1], projected[:, 2]
    product = (gate_b * values).astype(BF16)
    halo = halo_tokens.astype(F32)
    halo = (halo * inverse_rms(halo) * gain_in).astype(BF16)
    before = (dot(halo, w_in[:, 0]) * dot(halo, w_in[:, 2])).astype(BF16)[-2:]
    before = jnp.where(starts_seq, jnp.zeros_like(before), before)
    extended = jnp.concatenate([before, product], axis=0).astype(F32)
    conv_out = taps[0] * extended[:-2] + taps[1] * extended[1:-1] + taps[2] * extended[2:]
    gated = (gate_c * conv_out).astype(BF16)

    here = jnp.concatenate([mine(gated), swap_core(other(gated))], axis=1)
    there = swap_chip(here)
    w_here = jnp.concatenate([w_out, w_out_core], axis=0)
    w_there = jnp.concatenate([w_out_chip, w_out_chip_core], axis=0)
    middle = mine(tokens).astype(F32) + (dot(here, w_here) + dot(there, w_there))
    scale_ffn = inverse_rms(middle)
    unit_ffn = middle * scale_ffn
    ffn_own = (unit_ffn * gain_ffn).astype(BF16)
    ffn_other = swap_core(ffn_own)
    ffn_pair_own = swap_pair(ffn_own)
    ffn_pair_other = swap_core(ffn_pair_own)

    ffn_in = jnp.concatenate([ffn_own, ffn_other], axis=0)
    cot = jnp.concatenate([cot_own, cot_other], axis=0)
    act, grad_gate, grad_up = gates(ffn_in, cot, w_gate, w_up, w_down)
    back_part = dot_cols(grad_gate, w_gate) + dot_cols(grad_up, w_up)
    back_ffn = chip_sum(back_part.astype(BF16))
    down_part = dot(act, w_down).astype(BF16)

    ffn_in_pair = jnp.concatenate([ffn_pair_own, ffn_pair_other], axis=0)
    cot_pair = jnp.concatenate([cot_pair_own, cot_pair_other], axis=0)
    act_p, grad_gate_p, grad_up_p = gates(ffn_in_pair, cot_pair, w_gate, w_up, w_down)

    lines = Lines()
    piece = width // 4

    def columns(block, j):
        return lax.dynamic_slice_in_dim(block, pair * (2 * piece) + j * piece, piece, 1)

    down_t, gate_t, up_t = [], [], []
    for j in range(2):
        grad = dot_rows(act, columns(cot, j)) + dot_rows(act_p, columns(cot_pair, j))
        down_t.append(lines.total(grad.astype(BF16)))
    for out, own_g, pair_g in ((gate_t, grad_gate, grad_gate_p), (up_t, grad_up, grad_up_p)):
        for j in range(2):
            grad = dot_rows(columns(ffn_in, j), own_g) + dot_rows(columns(ffn_in_pair, j), pair_g)
            out.append(lines.total(grad.astype(BF16)))

    def widen(totals, axis):
        theirs = [swap_pair(t) for t in totals]
        low, high = zip(*((jnp.where(pair == 0, t, v), jnp.where(pair == 0, v, t)) for t, v in zip(totals, theirs)))
        return jnp.concatenate([*low, *high], axis=axis).astype(F32)

    total_down = widen(down_t, 1)
    total_gate_up = jnp.stack([widen(gate_t, 0), widen(up_t, 0)], axis=1)

    grad_mid, gain_ffn_term = norm_back(back_ffn, unit_ffn, scale_ffn, gain_ffn)
    grad_mid = grad_mid + cot_own.astype(F32)
    mid_own = grad_mid.astype(BF16)
    mid_low = in_order(mid_own, swap_core(mid_own))
    grad_w_out = dot_rows(gated, mid_low).astype(BF16)
    grad_gated = dot_cols(mid_low, w_out)
    grad_c = grad_gated * conv_out
    grad_conv_out = (grad_gated * gate_c).astype(BF16)
    after = neighbour(grad_conv_out[:2], -1)
    after = jnp.where(ends_seq, jnp.zeros_like(after), after)
    ext_grad = jnp.concatenate([grad_conv_out, after], axis=0).astype(F32)
    grad_product = taps[2] * ext_grad[:-2] + taps[1] * ext_grad[1:-1] + taps[0] * ext_grad[2:]
    grad_conv_f = grad_conv_out.astype(F32)
    grad_taps = jnp.concatenate(
        [jnp.sum(grad_conv_f * extended[k : k + rows], axis=0) for k in range(3)], axis=0
    )
    grad_proj = [
        (grad_product * values).astype(BF16),
        grad_c.astype(BF16),
        (grad_product * gate_b).astype(BF16),
    ]
    grad_proj = jnp.concatenate(grad_proj, axis=1)
    w_in_flat = jnp.concatenate([w_in[:, 0], w_in[:, 1], w_in[:, 2]], axis=1)
    back_in = dot_cols(grad_proj, w_in_flat).astype(BF16)
    back_in = chip_sum(jnp.concatenate([mine(back_in), other(back_in)], axis=0))
    own_inputs = mine(tokens).astype(F32)
    own_scale = inverse_rms(own_inputs)
    grad_in, gain_in_term = norm_back(back_in, own_inputs * own_scale, own_scale, gain_in)
    grad_own = (grad_in + grad_mid).astype(BF16)
    grad_tokens = in_order(grad_own, swap_core(grad_own))

    ffn_sum = chip_sum(down_part)
    out_own = (middle + ffn_sum).astype(BF16)
    layer_out = in_order(out_own, swap_core(out_own))

    grad_w_in = dot_rows(normed, grad_proj).astype(BF16)
    channels = w_in.shape[2]
    total_in = []
    for k in range(2):
        total_in.append(lines.total_pairs(grad_w_in[k * (width // 2) : (k + 1) * (width // 2)]))
    total_in = jnp.concatenate(total_in, axis=0).astype(F32)
    total_w_in = jnp.stack([total_in[:, k * channels : (k + 1) * channels] for k in range(3)], axis=1)
    gains = jnp.stack([gain_in_term, gain_ffn_term], axis=0)
    gains = (gains + swap_core(gains)).astype(BF16)
    small = jnp.zeros((32, width), BF16)
    small = small.at[:2].set(gains)
    small = small.at[2, : 3 * channels].set(grad_taps.astype(BF16))
    total_last = lines.total_pairs(jnp.concatenate([grad_w_out, small], axis=0)).astype(F32)
    n_out = w_out.shape[0]
    total_w_out = total_last[:n_out]
    total_gain_in = total_last[n_out]
    total_gain_ffn = total_last[n_out + 1]
    total_taps = total_last[n_out + 2, : 3 * channels].reshape(3, channels)
    return (
        layer_out,
        grad_tokens,
        total_gain_in,
        total_gain_ffn,
        total_w_in,
        total_taps,
        total_w_out,
        total_gate_up,
        total_down,
    )


def solution(mesh):
    placed = (
        P("seq", None),
        P(),
        P(None, None, "tensor"),
        P(None, "tensor"),
        P("tensor", None),
        P(),
        P(None, None, "tensor"),
        P("tensor", None),
        P("seq", None),
    )
    return jax.shard_map(
        shards,
        mesh=mesh,
        in_specs=placed,
        out_specs=(
            P("seq", None),
            P("seq", None),
            P(),
            P(),
            P(None, None, "tensor"),
            P(None, "tensor"),
            P("tensor", None),
            P(None, None, "tensor"),
            P("tensor", None),
        ),
        check_vma=False,
    )
```
